512 devices in a mesh: az: 16 (over z_hi, x, core), curve: 32 (over z_lo, y).
Axes of the slice: x: 4, y: 4, z: 16 (z_hi: 2, z_lo: 8; z = z_hi * 8 + z_lo), core: 2. Of those that a mesh axis runs over, the one named last changes fastest.
Arguments:
- fields: float32 [2, 256, 16, 4096], P(None, 'az', None, 'curve'), may hold values from -6 to 6
- impedance: float32 [2, 256, 4096], P(None, 'az', 'curve'), may hold values from 0.25 to 1.5
- tile_data: bfloat16 [256, 32, 3, 2, 128, 128], P('az', 'curve'), may hold values from -0.21875 to 0.21875
- tile_cols: int32 [256, 32, 3], P('az', 'curve'), may hold values from 0 to 31, as said below
- tile_count: int32 [256, 32], P('az', 'curve'), may hold values from 1 to 3
Outputs:
- applied: float32 [2, 256, 16, 4096], P(None, 'az', None, 'curve')
The draws below stay inside these ranges and needn't reach their ends.
Inputs may be any that keep to these rules, and one draw needn't show every extreme that they name: `tile_cols`: for every mode and block row the 3 entries are distinct blocks lying within one block of the row's own block along the closed curve, indices taken modulo 32; only the first tile_count entries are used.
All inputs are finite; a program needn't handle non-finite values.
Results may differ from the reference program's by a relative error of at most 0.0021.
Values may be sent and summed in bfloat16 or wider, within the bound.
A program may use at most 64 MiB of HBM per device.

```python
import jax
import jax.numpy as jnp
from jax import lax

NPHI = 256
RHS = 16
BLK = 128
TILES = 3
MODES = 256
NBLK = 32
NODES = 4096


def pattern_draw(key):
    base_key = jax.random.fold_in(key, 7)
    key_cols, key_count = jax.random.split(base_key)
    scores = jax.random.randint(key_cols, (MODES, NBLK, TILES), 0, 1 << 20) * TILES + jnp.arange(TILES, dtype=jnp.int32)
    ranking = jnp.argsort(scores, axis=-1, stable=True).astype(jnp.int32)
    block_rows = jnp.arange(NBLK, dtype=jnp.int32)[None, :, None]
    columns = jnp.mod(block_rows + ranking - 1, NBLK).astype(jnp.int32)
    counts = jax.random.randint(key_count, (MODES, NBLK), 1, TILES + 1).astype(jnp.int32)
    counts = counts.at[0, 0].set(TILES).at[0, 1].set(1)
    return (columns, counts)


def draw_tile_cols(key, part):
    return pattern_draw(key)[0]


def draw_tile_count(key, part):
    return pattern_draw(key)[1]


def block_levels(rng, shape, shards, least, high):
    factor_of, own = 1.0, jax.random.fold_in(rng, 6)
    for dim, blocks in shards:
        draws = jnp.exp(jax.random.uniform(jax.random.fold_in(own, dim), (blocks,), jnp.float32, least / len(shards), high / len(shards)))
        factor_of = factor_of * jnp.repeat(draws, shape[dim] // blocks).reshape([-1 if axis == dim else 1 for axis in range(len(shape))])
    return factor_of


def centred(stream_key, extent, scale, most, cuts=(), held_as=jnp.bfloat16):
    values = scale * jax.random.normal(stream_key, extent, jnp.float32)
    if cuts:
        values = values * block_levels(stream_key, extent, cuts, -0.22, 0.18)
    return jnp.clip(values, -most, most).astype(held_as)


def setup_inputs(seed: int = 0) -> dict:
    splits = jax.random.split(jax.random.key(seed), 6)
    fields = centred(splits[0], (2, NPHI, RHS, NODES), 1.0, 6.0, ((1, 16), (3, 32)), jnp.float32)
    impedance = jnp.clip(0.25 + 1.25 * jax.random.uniform(splits[1], (2, NPHI, NODES), jnp.float32) ** block_levels(splits[1], (2, NPHI, NODES), ((1, 16), (2, 32)), -0.2, 0.2), 0.25, 1.5)
    tile_data = centred(splits[2], (MODES, NBLK, TILES, 2, BLK, BLK), (6 * BLK) ** -0.5, 0.21875, ((0, 16), (1, 32)))
    tile_cols = draw_tile_cols(jax.random.fold_in(splits[5], 71), 0)
    tile_count = draw_tile_count(jax.random.fold_in(splits[5], 71), 0)
    return dict(fields=fields, impedance=impedance, tile_data=tile_data, tile_cols=tile_cols, tile_count=tile_count)


def reference(fields, impedance, tile_data, tile_cols, tile_count):
    period = fields.shape[1]
    rhs_count = fields.shape[2]
    node_count = fields.shape[3]
    block_size = tile_data.shape[-1]
    block_total = node_count // block_size
    slot_count = tile_data.shape[2]
    signal = fields[0] + 1j * fields[1]
    spectrum = jnp.fft.fft(signal, axis=0) / period
    mode_values = jnp.stack([jnp.real(spectrum), jnp.imag(spectrum)]).astype(jnp.bfloat16)
    blocked = jnp.transpose(mode_values.reshape(2, period, rhs_count, block_total, block_size), (1, 0, 2, 3, 4))

    def one_mode(inputs):
        vectors, matrices, columns, counts = inputs
        picked = vectors[:, :, columns, :].astype(jnp.float32)
        live_slots = (jnp.arange(slot_count, dtype=jnp.int32)[None, :] < counts[:, None]).astype(jnp.float32)
        picked = picked * live_slots[None, None, :, :, None]
        matrices = matrices.astype(jnp.float32)
        tile_real = matrices[:, :, 0]
        tile_imag = matrices[:, :, 1]

        def tile_apply(mat, vals):
            return jnp.einsum("btpq,rbtq->rbp", mat, vals)

        near_real = tile_apply(tile_real, picked[0]) - tile_apply(tile_imag, picked[1])
        near_imag = tile_apply(tile_real, picked[1]) + tile_apply(tile_imag, picked[0])
        return jnp.stack([near_real, near_imag])

    near = lax.map(one_mode, (blocked, tile_data, tile_cols, tile_count))
    near = near.reshape(period, 2, rhs_count, node_count)
    near_complex = near[:, 0] + 1j * near[:, 1]
    returned = jnp.fft.ifft(near_complex, axis=0) * period
    back_real = jnp.real(returned).astype(jnp.float32)
    back_imag = jnp.imag(returned).astype(jnp.float32)
    imped_real = impedance[0][:, None, :]
    imped_imag = impedance[1][:, None, :]
    out_real = fields[0] + imped_real * back_real - imped_imag * back_imag
    out_imag = fields[1] + imped_real * back_imag + imped_imag * back_real
    return jnp.stack([out_real, out_imag]).astype(jnp.float32)
```

```python
import functools
import math

import jax
import jax.numpy as jnp
import numpy as np
from jax import lax
from jax.experimental import pallas as pl
from jax.experimental.pallas import tpu as pltpu
from jax.sharding import PartitionSpec as P

MESH = pl.DeviceIdType.MESH
F32 = jnp.float32
BF16 = jnp.bfloat16
FIELD_SAME, FIELD_OTHER, MODE_OWN, MODE_OTHER, HALO_UP, HALO_DOWN, NEAR_SAME, NEAR_OTHER, BACK = range(9)
CHUNKS = 2
GROUPS = 8
LOCAL = 16


def transform_tables():
    period = 2 * GROUPS * LOCAL
    half_size = GROUPS * LOCAL
    tables = []
    for half in range(2):
        k = half * half_size + np.arange(half_size).reshape(GROUPS, 1, LOCAL)
        p = np.stack([side * half_size + np.arange(half_size) for side in (half, 1 - half)])
        p = p.reshape(2, GROUPS, 1, LOCAL)
        product = (k.reshape(-1, 1) * p.reshape(1, -1)) % period
        angle = 2.0 * math.pi / period * product
        cosine = np.cos(angle).reshape(GROUPS, LOCAL, 2, GROUPS, LOCAL)
        sine = np.sin(angle).reshape(GROUPS, LOCAL, 2, GROUPS, LOCAL)
        full = np.zeros((GROUPS, 2, LOCAL, 2, GROUPS, 2, LOCAL))
        full[:, 0, :, :, :, 0, :] = cosine
        full[:, 0, :, :, :, 1, :] = sine
        full[:, 1, :, :, :, 0, :] = -sine
        full[:, 1, :, :, :, 1, :] = cosine
        full = full.reshape(2 * half_size, 4 * half_size)
        high = full.astype(np.float32).astype(jnp.bfloat16)
        low = (full - high.astype(np.float64)).astype(np.float32).astype(jnp.bfloat16)
        tables.append(np.stack([high, low]))
    return np.stack(tables)


def dot(left, right):
    return jnp.dot(left, right, preferred_element_type=F32)


def split(value):
    high = value.astype(BF16)
    low = (value - high.astype(F32)).astype(BF16)
    return high, low


def kernel(
    fields_ref,
    imped_ref,
    cols_ref,
    count_ref,
    tiles_hbm,
    tables_hbm,
    out_ref,
    tiles,
    tables,
    stage,
    field_same,
    field_other,
    modes,
    window,
    spread,
    near,
    near_stage,
    near_same,
    near_other,
    back,
    returned,
    send_sem,
    recv_sem,
    load_sem,
):
    az = lax.axis_index("az")
    curve = lax.axis_index("curve")
    blocks = lax.axis_size("curve")
    half = az // GROUPS
    me = az % GROUPS
    base = half * GROUPS
    far = (1 - half) * GROUPS
    last = blocks - 1
    at_end = jnp.logical_or(curve == 0, curve == last)
    across = (az + GROUPS) % (2 * GROUPS)
    up = (jnp.where(curve == last, across, az), (curve + 1) % blocks)
    down = (jnp.where(curve == 0, across, az), (curve + last) % blocks)
    up_source = jnp.where(curve == last, 3, 1)
    down_source = jnp.where(curve == 0, 3, 1)

    def peer(step):
        return (me + step) % GROUPS

    barrier = pltpu.get_barrier_semaphore()
    for step in range(GROUPS):
        pl.semaphore_signal(barrier, inc=1, device_id=(far + peer(step), curve), device_id_type=MESH)
    for device in (up, down):
        pl.semaphore_signal(barrier, inc=1, device_id=device, device_id_type=MESH)
    for step in range(1, GROUPS):
        pl.semaphore_signal(barrier, inc=1, device_id=(base + peer(step), curve), device_id_type=MESH)

    table_load = pltpu.make_async_copy(tables_hbm, tables, load_sem.at[0])
    table_load.start()
    tile_load = pltpu.make_async_copy(tiles_hbm, tiles, load_sem.at[1])
    tile_load.start()

    def remote(source, target, row, chunk, device):
        pltpu.make_async_remote_copy(
            src_ref=source,
            dst_ref=target,
            send_sem=send_sem.at[row, chunk],
            recv_sem=recv_sem.at[row, chunk],
            device_id=device,
            device_id_type=MESH,
        ).start()

    def take(ref, row, chunk):
        pltpu.make_async_copy(ref, ref, recv_sem.at[row, chunk]).wait()

    def drain(ref, row, chunk):
        pltpu.make_async_copy(ref, ref, send_sem.at[row, chunk]).wait()

    def exchange(source, same, other, same_row, other_row, chunk):
        for step in range(GROUPS):
            group = peer(step)
            remote(source.at[chunk, group, 0], other.at[chunk, me], other_row, chunk, (far + group, curve))
        for step in range(1, GROUPS):
            group = peer(step)
            remote(source.at[chunk, group], same.at[chunk, :, me], same_row, chunk, (base + group, curve))
        same[chunk, 0, me] = source[chunk, me, 0]
        same[chunk, 1, me] = source[chunk, me, 1]

    def rows_of(value):
        return value.reshape(GROUPS * 2 * LOCAL, value.shape[-1])

    width = GROUPS * 2 * LOCAL

    def transform_same(same, chunk, side, first):
        columns = pl.ds(first * width, width)
        high = rows_of(same[chunk, 0])
        low = rows_of(same[chunk, 1])
        return (
            dot(tables[side, 0, :, columns], high)
            + dot(tables[side, 0, :, columns], low)
            + dot(tables[side, 1, :, columns], high)
        )

    def transform_other(other, chunk, side, first):
        columns = pl.ds(first * width, width)
        high = rows_of(other[chunk])
        return dot(tables[side, 0, :, columns], high) + dot(tables[side, 1, :, columns], high)

    for chunk in range(CHUNKS):
        for group in range(GROUPS):
            rows = fields_ref[pl.ds(group + GROUPS * chunk, 2 * LOCAL, stride=CHUNKS * GROUPS), :]
            high, low = split(rows)
            stage[chunk, group, 0] = high
            stage[chunk, group, 1] = low

    pl.semaphore_wait(barrier, 2 * GROUPS + 1)
    for chunk in range(CHUNKS):
        exchange(stage, field_same, field_other, FIELD_SAME, FIELD_OTHER, chunk)
    table_load.wait()

    def forward(chunk):
        take(field_same.at[chunk, :, pl.ds(0, GROUPS - 1)], FIELD_SAME, chunk)
        total = transform_same(field_same, chunk, half, 0)
        take(field_other.at[chunk], FIELD_OTHER, chunk)
        total = total + transform_other(field_other, chunk, half, 1)
        scale = 1.0 / (2 * GROUPS * LOCAL)
        modes[chunk, 0] = (total * scale).astype(BF16).reshape(modes.shape[2:])
        for step in range(1, GROUPS):
            group = peer(step)
            remote(modes.at[chunk, 0, group], window.at[chunk, 1, me], MODE_OWN, chunk, (base + group, curve))
        window[chunk, 1, me] = modes[chunk, 0, me]

        @pl.when(at_end)
        def _():
            wrapped = transform_same(field_same, chunk, 1 - half, 1)
            wrapped = wrapped + transform_other(field_other, chunk, 1 - half, 0)
            modes[chunk, 1] = (wrapped * scale).astype(BF16).reshape(modes.shape[2:])
            for step in range(1, GROUPS):
                group = peer(step)
                remote(modes.at[chunk, 1, group], window.at[chunk, 3, me], MODE_OTHER, chunk, (base + group, curve))
            window[chunk, 3, me] = modes[chunk, 1, me]

    def halo(chunk):
        take(window.at[chunk, 1, pl.ds(0, GROUPS - 1)], MODE_OWN, chunk)

        @pl.when(at_end)
        def _():
            take(window.at[chunk, 3, pl.ds(0, GROUPS - 1)], MODE_OTHER, chunk)

        remote(window.at[chunk, up_source], window.at[chunk, 0], HALO_UP, chunk, up)
        remote(window.at[chunk, down_source], window.at[chunk, 2], HALO_DOWN, chunk, down)

    def slot_of(mode, place):
        block = (curve + place + last) % blocks
        slot = jnp.where(cols_ref[mode, 0] == block, 0, jnp.where(cols_ref[mode, 1] == block, 1, 2))
        return slot, jnp.where(slot < count_ref[mode], 1.0, 0.0).astype(F32)

    def product(mode, place):
        slot, weight = slot_of(mode, place)
        real = spread[place, pl.ds(mode, GROUPS, stride=2 * LOCAL), :] * weight
        imag = spread[place, pl.ds(mode + LOCAL, GROUPS, stride=2 * LOCAL), :] * -weight
        left = jnp.concatenate([real, imag], axis=0)
        right = jnp.concatenate([imag, -real], axis=0)
        both = jnp.concatenate([left, right], axis=1).astype(BF16)
        tile = jnp.concatenate([tiles[mode, slot, 0], tiles[mode, slot, 1]], axis=1)
        return lax.dot_general(both, tile, (((1,), (1,)), ((), ())), preferred_element_type=F32)

    unroll = 4

    def near_own(chunk):
        spread[1] = rows_of(window[chunk, 1]).astype(F32)

        def body(index, carry):
            for inner in range(unroll):
                mode = index * unroll + inner
                total = product(mode, 1)
                near[chunk, pl.ds(mode, GROUPS, stride=2 * LOCAL), :] = total[:GROUPS]
                near[chunk, pl.ds(mode + LOCAL, GROUPS, stride=2 * LOCAL), :] = total[GROUPS:]
            return carry

        lax.fori_loop(0, LOCAL // unroll, body, 0)

    def near_rest(chunk):
        take(window.at[chunk, 0], HALO_UP, chunk)
        take(window.at[chunk, 2], HALO_DOWN, chunk)
        spread[0] = rows_of(window[chunk, 0]).astype(F32)
        spread[2] = rows_of(window[chunk, 2]).astype(F32)

        def body(index, carry):
            for inner in range(unroll):
                mode = index * unroll + inner
                total = product(mode, 0) + product(mode, 2)
                real = pl.ds(mode, GROUPS, stride=2 * LOCAL)
                imag = pl.ds(mode + LOCAL, GROUPS, stride=2 * LOCAL)
                near[chunk, real, :] = near[chunk, real, :] + total[:GROUPS]
                near[chunk, imag, :] = near[chunk, imag, :] + total[GROUPS:]
            return carry

        lax.fori_loop(0, LOCAL // unroll, body, 0)
        high, low = split(near[chunk])
        near_stage[chunk, :, 0] = high.reshape(GROUPS, 2 * LOCAL, high.shape[-1])
        near_stage[chunk, :, 1] = low.reshape(GROUPS, 2 * LOCAL, low.shape[-1])
        exchange(near_stage, near_same, near_other, NEAR_SAME, NEAR_OTHER, chunk)

    def inverse(chunk):
        take(near_same.at[chunk, :, pl.ds(0, GROUPS - 1)], NEAR_SAME, chunk)
        total = transform_same(near_same, chunk, half, 0)
        take(near_other.at[chunk], NEAR_OTHER, chunk)
        total = total + transform_other(near_other, chunk, half, 1)
        back[chunk] = total.reshape(back.shape[1:])
        for step in range(1, GROUPS):
            group = peer(step)
            target = returned.at[chunk, pl.ds(pl.multiple_of(me * 2 * LOCAL, 2 * LOCAL), 2 * LOCAL)]
            remote(back.at[chunk, group], target, BACK, chunk, (base + group, curve))
        returned[chunk, pl.ds(pl.multiple_of(me * 2 * LOCAL, 2 * LOCAL), 2 * LOCAL)] = back[chunk, me]

    def combine(chunk):
        take(returned.at[chunk, pl.ds(0, (GROUPS - 1) * 2 * LOCAL)], BACK, chunk)
        for point in range(LOCAL):
            real = returned[chunk, pl.ds(point, GROUPS, stride=2 * LOCAL), :]
            minus_imag = returned[chunk, pl.ds(point + LOCAL, GROUPS, stride=2 * LOCAL), :]
            imped_real = imped_ref[pl.ds(point, 1), :]
            imped_imag = imped_ref[pl.ds(point + LOCAL, 1), :]
            row = point * CHUNKS * GROUPS + chunk * GROUPS
            rows = pl.ds(row, GROUPS)
            out_ref[rows, :] = fields_ref[rows, :] + imped_real * real + imped_imag * minus_imag
            rows = pl.ds(row + LOCAL * CHUNKS * GROUPS, GROUPS)
            out_ref[rows, :] = fields_ref[rows, :] - imped_real * minus_imag + imped_imag * real

    forward(0)
    halo(0)
    forward(1)
    tile_load.wait()
    near_own(0)
    halo(1)
    near_rest(0)
    near_own(1)
    near_rest(1)
    inverse(0)
    inverse(1)
    combine(0)
    combine(1)

    for chunk in range(CHUNKS):
        drain(field_same.at[chunk, :, pl.ds(0, GROUPS - 1)], FIELD_SAME, chunk)
        drain(field_other.at[chunk], FIELD_OTHER, chunk)
        drain(window.at[chunk, 1, pl.ds(0, GROUPS - 1)], MODE_OWN, chunk)

        @pl.when(at_end)
        def _():
            drain(window.at[chunk, 3, pl.ds(0, GROUPS - 1)], MODE_OTHER, chunk)

        drain(window.at[chunk, 0], HALO_UP, chunk)
        drain(window.at[chunk, 2], HALO_DOWN, chunk)
        drain(near_same.at[chunk, :, pl.ds(0, GROUPS - 1)], NEAR_SAME, chunk)
        drain(near_other.at[chunk], NEAR_OTHER, chunk)
        drain(returned.at[chunk, pl.ds(0, (GROUPS - 1) * 2 * LOCAL)], BACK, chunk)


def on_device(tables, fields, impedance, tile_data, tile_cols, tile_count):
    points, rhs, nodes = fields.shape[1:]
    block = tile_data.shape[-1]
    modes, _, slots = tile_data.shape[:3]
    pair = 2 * LOCAL
    whole = GROUPS * pair
    vmem = pl.BlockSpec(memory_space=pltpu.VMEM)
    smem = pl.BlockSpec(memory_space=pltpu.SMEM)
    hbm = pl.BlockSpec(memory_space=pl.ANY)
    out = pl.pallas_call(
        kernel,
        out_shape=jax.ShapeDtypeStruct((2 * points * rhs, nodes), F32),
        in_specs=[vmem, vmem, smem, smem, hbm, hbm],
        out_specs=vmem,
        scratch_shapes=[
            pltpu.VMEM((modes, slots, 2, block, block), BF16),
            pltpu.VMEM(tables.shape, BF16),
            pltpu.VMEM((CHUNKS, GROUPS, 2, pair, nodes), BF16),
            pltpu.VMEM((CHUNKS, 2, GROUPS, pair, nodes), BF16),
            pltpu.VMEM((CHUNKS, GROUPS, pair, nodes), BF16),
            pltpu.VMEM((CHUNKS, 2, GROUPS, pair, nodes), BF16),
            pltpu.VMEM((CHUNKS, 4, GROUPS, pair, nodes), BF16),
            pltpu.VMEM((3, whole, nodes), F32),
            pltpu.VMEM((CHUNKS, whole, nodes), F32),
            pltpu.VMEM((CHUNKS, GROUPS, 2, pair, nodes), BF16),
            pltpu.VMEM((CHUNKS, 2, GROUPS, pair, nodes), BF16),
            pltpu.VMEM((CHUNKS, GROUPS, pair, nodes), BF16),
            pltpu.VMEM((CHUNKS, GROUPS, pair, nodes), F32),
            pltpu.VMEM((CHUNKS, whole, nodes), F32),
            pltpu.SemaphoreType.DMA((9, CHUNKS)),
            pltpu.SemaphoreType.DMA((9, CHUNKS)),
            pltpu.SemaphoreType.DMA((2,)),
        ],
        compiler_params=pltpu.CompilerParams(collective_id=0, has_side_effects=True),
    )(
        fields.reshape(2 * points * rhs, nodes),
        impedance.reshape(2 * points, nodes),
        tile_cols.reshape(modes, slots),
        tile_count.reshape(modes),
        tile_data.reshape(modes, slots, 2, block, block),
        tables,
    )
    return out.reshape(fields.shape)


def solution(mesh):
    placed = (
        P(None, "az", None, "curve"),
        P(None, "az", "curve"),
        P("az", "curve", None, None, None, None),
        P("az", "curve", None),
        P("az", "curve"),
    )

    def apply(*arrays):
        tables = jnp.asarray(transform_tables())
        return jax.shard_map(
            on_device,
            mesh=mesh,
            in_specs=(P(),) + placed,
            out_specs=P(None, "az", None, "curve"),
            check_vma=False,
        )(tables, *arrays)

    return apply
```

```python
import functools
import math

import jax
import jax.numpy as jnp
import numpy as np
from jax import lax
from jax.experimental import pallas as pl
from jax.experimental.pallas import tpu as pltpu
from jax.sharding import PartitionSpec as P

MESH = pl.DeviceIdType.MESH
F32 = jnp.float32
BF16 = jnp.bfloat16
FIELD, FIELD_OTHER, MODE_OWN, MODE_OTHER, PART, FAR_PART, WRAP_PART, WRAP_FAR = range(8)
HALO_UP, HALO_DOWN, NEAR_SAME, NEAR_OTHER, BACK, BACK_FAR = range(8, 14)
CHUNKS = 2
GROUPS = 8
LOCAL = 16


def transform_tables():
    period = 2 * GROUPS * LOCAL
    half_size = GROUPS * LOCAL
    tables = []
    for half in range(2):
        k = half * half_size + np.arange(half_size).reshape(GROUPS, 1, LOCAL)
        p = np.stack([side * half_size + np.arange(half_size) for side in (half, 1 - half)])
        p = p.reshape(2, GROUPS, 1, LOCAL)
        product = (k.reshape(-1, 1) * p.reshape(1, -1)) % period
        angle = 2.0 * math.pi / period * product
        cosine = np.cos(angle).reshape(GROUPS, LOCAL, 2, GROUPS, LOCAL)
        sine = np.sin(angle).reshape(GROUPS, LOCAL, 2, GROUPS, LOCAL)
        full = np.zeros((GROUPS, 2, LOCAL, 2, GROUPS, 2, LOCAL))
        full[:, 0, :, :, :, 0, :] = cosine
        full[:, 0, :, :, :, 1, :] = sine
        full[:, 1, :, :, :, 0, :] = -sine
        full[:, 1, :, :, :, 1, :] = cosine
        full = full.reshape(2 * half_size, 4 * half_size)
        high = full.astype(np.float32).astype(jnp.bfloat16)
        low = (full - high.astype(np.float64)).astype(np.float32).astype(jnp.bfloat16)
        tables.append(np.stack([high, low]))
    return np.stack(tables)


def dot(left, right):
    return jnp.dot(left, right, preferred_element_type=F32)


def split(value):
    high = value.astype(BF16)
    low = (value - high.astype(F32)).astype(BF16)
    return high, low


def kernel(
    fields_hbm,
    imped_ref,
    cols_ref,
    count_ref,
    tiles_hbm,
    tables_hbm,
    out,
    fields,
    tiles,
    turned,
    tables,
    stage,
    field_same,
    field_other,
    modes,
    part,
    far_part,
    part_in,
    far_in,
    window,
    spread,
    near,
    near_stage,
    near_same,
    near_other,
    back,
    returned,
    back_far,
    returned_far,
    send_sem,
    recv_sem,
    load_sem,
):
    az = lax.axis_index("az")
    curve = lax.axis_index("curve")
    blocks = lax.axis_size("curve")
    half = az // GROUPS
    me = az % GROUPS
    base = half * GROUPS
    far = (1 - half) * GROUPS
    last = blocks - 1
    at_end = jnp.logical_or(curve == 0, curve == last)
    across = (az + GROUPS) % (2 * GROUPS)
    up = (jnp.where(curve == last, across, az), (curve + 1) % blocks)
    down = (jnp.where(curve == 0, across, az), (curve + last) % blocks)
    up_source = jnp.where(curve == last, 3, 1)
    down_source = jnp.where(curve == 0, 3, 1)

    def peer(step):
        return (me + step) % GROUPS

    barrier = pltpu.get_barrier_semaphore()
    greeted = [(far + peer(step), curve) for step in range(GROUPS)]
    greeted += [up, down] + [(base + peer(step), curve) for step in range(1, GROUPS)]
    for device in greeted:
        pl.semaphore_signal(barrier, inc=1, device_id=device, device_id_type=MESH)

    def field_load(chunk):
        rows = pl.ds(chunk * GROUPS, GROUPS)
        return pltpu.make_async_copy(fields_hbm.at[:, rows], fields.at[chunk], load_sem.at[5 + chunk])

    for chunk in range(CHUNKS):
        field_load(chunk).start()
    table_load = pltpu.make_async_copy(tables_hbm, tables, load_sem.at[1])
    table_load.start()
    tile_load = pltpu.make_async_copy(tiles_hbm, tiles, load_sem.at[2])
    tile_load.start()

    def remote(source, target, row, chunk, device):
        pltpu.make_async_remote_copy(
            src_ref=source,
            dst_ref=target,
            send_sem=send_sem.at[row, chunk],
            recv_sem=recv_sem.at[row, chunk],
            device_id=device,
            device_id_type=MESH,
        ).start()

    def take(ref, row, chunk):
        pltpu.make_async_copy(ref, ref, recv_sem.at[row, chunk]).wait()

    def drain(ref, row, chunk):
        pltpu.make_async_copy(ref, ref, send_sem.at[row, chunk]).wait()

    def send_same(source, same, row, chunk):
        for step in range(1, GROUPS):
            group = peer(step)
            remote(source.at[chunk, group], same.at[chunk, :, me], row, chunk, (base + group, curve))
        same[chunk, 0, me] = source[chunk, me, 0]
        same[chunk, 1, me] = source[chunk, me, 1]

    def send_other(source, other, row, chunk):
        for step in range(GROUPS):
            group = peer(step)
            remote(source.at[chunk, group, 0], other.at[me], row, chunk, (far + group, curve))

    def rows_of(value):
        return value.reshape(GROUPS * 2 * LOCAL, value.shape[-1])

    width = GROUPS * 2 * LOCAL

    def transform_same(same, chunk, side, first):
        columns = pl.ds(first * width, width)
        high = rows_of(same[chunk, 0])
        low = rows_of(same[chunk, 1])
        return (
            dot(tables[side, 0, :, columns], high)
            + dot(tables[side, 0, :, columns], low)
            + dot(tables[side, 1, :, columns], high)
        )

    def transform_other(other, side, first):
        columns = pl.ds(first * width, width)
        high = rows_of(other[...])
        return dot(tables[side, 0, :, columns], high) + dot(tables[side, 1, :, columns], high)

    def fill(chunk):
        field_load(chunk).wait()
        for group in range(GROUPS):
            high, low = split(fields[chunk, :, group, :])
            stage[chunk, group, 0] = high
            stage[chunk, group, 1] = low

    fill(0)
    fill(1)
    pl.semaphore_wait(barrier, len(greeted))
    send_other(stage, field_other, FIELD_OTHER, 0)
    send_same(stage, field_same, FIELD, 1)
    send_same(stage, field_same, FIELD, 0)
    table_load.wait()

    def send_far(kind, row, chunk):
        for step in range(GROUPS):
            group = peer(step)
            remote(far_part.at[chunk, kind, group], far_in.at[chunk, kind, me], row, chunk, (far + group, curve))

    def send_near(kind, row, chunk):
        for step in range(1, GROUPS):
            group = peer(step)
            remote(part.at[chunk, kind, group], part_in.at[chunk, kind, me], row, chunk, (base + group, curve))
        part_in[chunk, kind, me] = part[chunk, kind, me]

    scale = 1.0 / (2 * GROUPS * LOCAL)

    def send_modes(total, kind, place, row, chunk):
        modes[kind] = (total * scale).astype(BF16).reshape(modes.shape[1:])
        for step in range(1, GROUPS):
            group = peer(step)
            remote(modes.at[kind, group], window.at[chunk, place, me], row, chunk, (base + group, curve))
        window[chunk, place, me] = modes[kind, me]

    def forward_first(chunk):
        take(field_same.at[chunk, :, pl.ds(0, GROUPS - 1)], FIELD, chunk)
        total = transform_same(field_same, chunk, half, 0)
        take(field_other, FIELD_OTHER, chunk)
        send_modes(total + transform_other(field_other, half, 1), 0, 1, MODE_OWN, chunk)

        @pl.when(at_end)
        def _():
            wrapped = transform_same(field_same, chunk, 1 - half, 1) + transform_other(field_other, 1 - half, 0)
            send_modes(wrapped, 1, 3, MODE_OTHER, chunk)

    def forward_last(chunk):
        take(field_same.at[chunk, :, pl.ds(0, GROUPS - 1)], FIELD, chunk)
        theirs = transform_same(field_same, chunk, 1 - half, 1)
        far_part[chunk, 0] = theirs.astype(BF16).reshape(far_part.shape[2:])
        send_far(0, FAR_PART, chunk)
        ours = transform_same(field_same, chunk, half, 0)
        part[chunk, 0] = ours.reshape(part.shape[2:])
        send_near(0, PART, chunk)

        @pl.when(at_end)
        def _():
            far_part[chunk, 1] = part[chunk, 0].astype(BF16)
            send_far(1, WRAP_FAR, chunk)
            part[chunk, 1] = theirs.reshape(part.shape[2:])
            send_near(1, WRAP_PART, chunk)

    def settle(chunk, kind, place):
        total = part_in[chunk, kind] + far_in[chunk, kind].astype(F32)
        window[chunk, place] = (total * scale).astype(BF16)

    def halo(chunk):
        if chunk == 0:
            take(window.at[chunk, 1, pl.ds(0, GROUPS - 1)], MODE_OWN, chunk)

            @pl.when(at_end)
            def _():
                take(window.at[chunk, 3, pl.ds(0, GROUPS - 1)], MODE_OTHER, chunk)
        else:
            take(part_in.at[chunk, 0, pl.ds(0, GROUPS - 1)], PART, chunk)
            take(far_in.at[chunk, 0], FAR_PART, chunk)
            settle(chunk, 0, 1)

            @pl.when(at_end)
            def _():
                take(part_in.at[chunk, 1, pl.ds(0, GROUPS - 1)], WRAP_PART, chunk)
                take(far_in.at[chunk, 1], WRAP_FAR, chunk)
                settle(chunk, 1, 3)

        remote(window.at[chunk, up_source], window.at[chunk, 0], HALO_UP, chunk, up)
        remote(window.at[chunk, down_source], window.at[chunk, 2], HALO_DOWN, chunk, down)

    def slot_of(mode, place):
        block = (curve + place + last) % blocks
        slot = jnp.where(cols_ref[0, 0, mode] == block, 0, jnp.where(cols_ref[1, 0, mode] == block, 1, 2))
        return slot, jnp.where(slot < count_ref[mode], 1.0, 0.0).astype(F32)

    def prepare():
        def body(mode, carry):
            for index, place in enumerate((1, 0, 2)):
                slot, weight = slot_of(mode, place)
                for kind in range(2):
                    tile = tiles[mode, slot, kind].astype(F32) * weight
                    turned[mode, index, kind] = jnp.transpose(tile).astype(BF16)
            return carry

        lax.fori_loop(0, LOCAL, body, 0)

    def spectrum_rows(mode, place):
        real = spread[place, pl.ds(mode, GROUPS, stride=2 * LOCAL), :]
        minus_imag = -spread[place, pl.ds(mode + LOCAL, GROUPS, stride=2 * LOCAL), :]
        left = jnp.concatenate([real, minus_imag], axis=0)
        right = jnp.concatenate([minus_imag, -real], axis=0)
        return [left.astype(BF16), right.astype(BF16)]

    def product(mode, places, first):
        left = jnp.concatenate([part for place in places for part in spectrum_rows(mode, place)], axis=1)
        right = turned[mode, pl.ds(first, len(places))]
        return dot(left, right.reshape(left.shape[1], right.shape[-1]))

    unroll = 4

    def near_own(chunk):
        spread[1] = rows_of(window[chunk, 1]).astype(F32)

        def body(index, carry):
            for inner in range(unroll):
                mode = index * unroll + inner
                total = product(mode, (1,), 0)
                near[chunk, pl.ds(mode, GROUPS, stride=2 * LOCAL), :] = total[:GROUPS]
                near[chunk, pl.ds(mode + LOCAL, GROUPS, stride=2 * LOCAL), :] = total[GROUPS:]
            return carry

        lax.fori_loop(0, LOCAL // unroll, body, 0)

    def near_rest(chunk):
        take(window.at[chunk, 0], HALO_UP, chunk)
        take(window.at[chunk, 2], HALO_DOWN, chunk)
        spread[0] = rows_of(window[chunk, 0]).astype(F32)
        spread[2] = rows_of(window[chunk, 2]).astype(F32)

        def body(index, carry):
            for inner in range(unroll):
                mode = index * unroll + inner
                total = product(mode, (0, 2), 1)
                real = pl.ds(mode, GROUPS, stride=2 * LOCAL)
                imag = pl.ds(mode + LOCAL, GROUPS, stride=2 * LOCAL)
                near[chunk, real, :] = near[chunk, real, :] + total[:GROUPS]
                near[chunk, imag, :] = near[chunk, imag, :] + total[GROUPS:]
            return carry

        lax.fori_loop(0, LOCAL // unroll, body, 0)
        high, low = split(near[chunk])
        near_stage[chunk, :, 0] = high.reshape(GROUPS, 2 * LOCAL, high.shape[-1])
        near_stage[chunk, :, 1] = low.reshape(GROUPS, 2 * LOCAL, low.shape[-1])
        if chunk == 0:
            send_other(near_stage, near_other, NEAR_OTHER, chunk)
            send_same(near_stage, near_same, NEAR_SAME, chunk)
        else:
            send_same(near_stage, near_same, NEAR_SAME, chunk)

    mine = pl.ds(pl.multiple_of(me * 2 * LOCAL, 2 * LOCAL), 2 * LOCAL)

    def send_back(total, chunk):
        back[chunk] = total.reshape(back.shape[1:])
        for step in range(1, GROUPS):
            group = peer(step)
            remote(back.at[chunk, group], returned.at[chunk, mine], BACK, chunk, (base + group, curve))
        returned[chunk, mine] = back[chunk, me]

    def inverse_first(chunk):
        take(near_same.at[chunk, :, pl.ds(0, GROUPS - 1)], NEAR_SAME, chunk)
        total = transform_same(near_same, chunk, half, 0)
        take(near_other, NEAR_OTHER, chunk)
        send_back(total + transform_other(near_other, half, 1), chunk)

    def inverse_last(chunk):
        take(near_same.at[chunk, :, pl.ds(0, GROUPS - 1)], NEAR_SAME, chunk)
        theirs = transform_same(near_same, chunk, 1 - half, 1)
        back_far[...] = theirs.astype(BF16).reshape(back_far.shape)
        for step in range(GROUPS):
            group = peer(step)
            remote(back_far.at[group], returned_far.at[me], BACK_FAR, chunk, (far + group, curve))
        send_back(transform_same(near_same, chunk, half, 0), chunk)

    def combine(chunk):
        take(returned.at[chunk, pl.ds(0, (GROUPS - 1) * 2 * LOCAL)], BACK, chunk)
        if chunk > 0:
            take(returned_far, BACK_FAR, chunk)
            returned[chunk] = returned[chunk] + rows_of(returned_far[...]).astype(F32)
        for point in range(LOCAL):
            real = returned[chunk, pl.ds(point, GROUPS, stride=2 * LOCAL), :]
            minus_imag = returned[chunk, pl.ds(point + LOCAL, GROUPS, stride=2 * LOCAL), :]
            imped_real = imped_ref[pl.ds(point, 1), :]
            imped_imag = imped_ref[pl.ds(point + LOCAL, 1), :]
            rows = pl.ds(chunk * GROUPS, GROUPS)
            out[point, rows, :] = imped_real * real + imped_imag * minus_imag
            out[point + LOCAL, rows, :] = imped_imag * real - imped_real * minus_imag

    forward_last(1)
    tile_load.wait()
    prepare()
    forward_first(0)
    halo(0)
    halo(1)
    near_own(0)
    near_own(1)
    near_rest(0)
    near_rest(1)
    inverse_last(1)
    inverse_first(0)
    combine(0)
    combine(1)

    drain(field_other, FIELD_OTHER, 0)
    drain(window.at[0, 1, pl.ds(0, GROUPS - 1)], MODE_OWN, 0)
    drain(far_in.at[1, 0], FAR_PART, 1)
    drain(part_in.at[1, 0, pl.ds(0, GROUPS - 1)], PART, 1)

    @pl.when(at_end)
    def _():
        drain(window.at[0, 3, pl.ds(0, GROUPS - 1)], MODE_OTHER, 0)
        drain(far_in.at[1, 1], WRAP_FAR, 1)
        drain(part_in.at[1, 1, pl.ds(0, GROUPS - 1)], WRAP_PART, 1)

    for chunk in range(CHUNKS):
        drain(field_same.at[chunk, :, pl.ds(0, GROUPS - 1)], FIELD, chunk)
        drain(window.at[chunk, 0], HALO_UP, chunk)
        drain(window.at[chunk, 2], HALO_DOWN, chunk)
        drain(near_same.at[chunk, :, pl.ds(0, GROUPS - 1)], NEAR_SAME, chunk)
        if chunk == 0:
            drain(near_other, NEAR_OTHER, chunk)
        else:
            drain(returned_far, BACK_FAR, chunk)
        drain(returned.at[chunk, pl.ds(0, (GROUPS - 1) * 2 * LOCAL)], BACK, chunk)


def on_device(tables, fields, impedance, tile_data, tile_cols, tile_count):
    points, rhs, nodes = fields.shape[1:]
    block = tile_data.shape[-1]
    modes, _, slots = tile_data.shape[:3]
    pair = 2 * LOCAL
    whole = GROUPS * pair
    vmem = pl.BlockSpec(memory_space=pltpu.VMEM)
    smem = pl.BlockSpec(memory_space=pltpu.SMEM)
    hbm = pl.BlockSpec(memory_space=pl.ANY)
    out = pl.pallas_call(
        kernel,
        out_shape=pltpu.VMEM((2 * points, rhs, nodes), F32),
        in_specs=[hbm, vmem, smem, smem, hbm, hbm],
        out_specs=vmem,
        scratch_shapes=[
            pltpu.VMEM((CHUNKS, 2 * points, GROUPS, nodes), F32),
            pltpu.VMEM((modes, slots, 2, block, block), BF16),
            pltpu.VMEM((modes, slots, 2, block, block), BF16),
            pltpu.VMEM(tables.shape, BF16),
            pltpu.VMEM((CHUNKS, GROUPS, 2, pair, nodes), BF16),
            pltpu.VMEM((CHUNKS, 2, GROUPS, pair, nodes), BF16),
            pltpu.VMEM((GROUPS, pair, nodes), BF16),
            pltpu.VMEM((2, GROUPS, pair, nodes), BF16),
            pltpu.VMEM((CHUNKS, 2, GROUPS, pair, nodes), F32),
            pltpu.VMEM((CHUNKS, 2, GROUPS, pair, nodes), BF16),
            pltpu.VMEM((CHUNKS, 2, GROUPS, pair, nodes), F32),
            pltpu.VMEM((CHUNKS, 2, GROUPS, pair, nodes), BF16),
            pltpu.VMEM((CHUNKS, 4, GROUPS, pair, nodes), BF16),
            pltpu.VMEM((3, whole, nodes), F32),
            pltpu.VMEM((CHUNKS, whole, nodes), F32),
            pltpu.VMEM((CHUNKS, GROUPS, 2, pair, nodes), BF16),
            pltpu.VMEM((CHUNKS, 2, GROUPS, pair, nodes), BF16),
            pltpu.VMEM((GROUPS, pair, nodes), BF16),
            pltpu.VMEM((CHUNKS, GROUPS, pair, nodes), F32),
            pltpu.VMEM((CHUNKS, whole, nodes), F32),
            pltpu.VMEM((GROUPS, pair, nodes), BF16),
            pltpu.VMEM((GROUPS, pair, nodes), BF16),
            pltpu.SemaphoreType.DMA((14, CHUNKS)),
            pltpu.SemaphoreType.DMA((14, CHUNKS)),
            pltpu.SemaphoreType.DMA((3 + 2 * CHUNKS,)),
        ],
        compiler_params=pltpu.CompilerParams(collective_id=0, has_side_effects=True),
    )(
        fields.reshape(2 * points, rhs, nodes),
        impedance.reshape(2 * points, nodes),
        jnp.transpose(tile_cols, (2, 1, 0)),
        tile_count.reshape(modes),
        tile_data.reshape(modes, slots, 2, block, block),
        tables,
    )
    return fields + out.reshape(fields.shape)


def solution(mesh):
    placed = (
        P(None, "az", None, "curve"),
        P(None, "az", "curve"),
        P("az", "curve", None, None, None, None),
        P("az", "curve", None),
        P("az", "curve"),
    )

    def apply(*arrays):
        tables = jnp.asarray(transform_tables())
        return jax.shard_map(
            on_device,
            mesh=mesh,
            in_specs=(P(),) + placed,
            out_specs=P(None, "az", None, "curve"),
            check_vma=False,
        )(tables, *arrays)

    return apply
```

```python
import functools
import math

import jax
import jax.numpy as jnp
import numpy as np
from jax import lax
from jax.experimental import pallas as pl
from jax.experimental.pallas import tpu as pltpu
from jax.sharding import PartitionSpec as P

MESH = pl.DeviceIdType.MESH
F32 = jnp.float32
BF16 = jnp.bfloat16
FIELD, FIELD_OTHER, MODE_OWN, PART, FAR_PART = range(5)
HALO_UP, HALO_DOWN, NEAR_SAME, NEAR_OTHER, BACK, BACK_FAR = range(5, 11)
CHUNKS = 2
GROUPS = 8
LOCAL = 16


def transform_tables():
    period = 2 * GROUPS * LOCAL
    half_size = GROUPS * LOCAL
    tables = []
    for half in range(2):
        k = half * half_size + np.arange(half_size).reshape(GROUPS, 1, LOCAL)
        p = np.stack([side * half_size + np.arange(half_size) for side in (half, 1 - half)])
        p = p.reshape(2, GROUPS, 1, LOCAL)
        product = (k.reshape(-1, 1) * p.reshape(1, -1)) % period
        angle = 2.0 * math.pi / period * product
        cosine = np.cos(angle).reshape(GROUPS, LOCAL, 2, GROUPS, LOCAL)
        sine = np.sin(angle).reshape(GROUPS, LOCAL, 2, GROUPS, LOCAL)
        full = np.zeros((GROUPS, 2, LOCAL, 2, GROUPS, 2, LOCAL))
        full[:, 0, :, :, :, 0, :] = cosine
        full[:, 0, :, :, :, 1, :] = sine
        full[:, 1, :, :, :, 0, :] = -sine
        full[:, 1, :, :, :, 1, :] = cosine
        full = full.reshape(2 * half_size, 4 * half_size)
        high = full.astype(np.float32).astype(jnp.bfloat16)
        low = (full - high.astype(np.float64)).astype(np.float32).astype(jnp.bfloat16)
        tables.append(np.stack([high, low]))
    return np.stack(tables)


def dot(left, right):
    return jnp.dot(left, right, preferred_element_type=F32)


def split(value):
    high = value.astype(BF16)
    low = (value - high.astype(F32)).astype(BF16)
    return high, low


def kernel(
    fields_hbm,
    imped_ref,
    cols_ref,
    count_ref,
    tiles_hbm,
    tables_hbm,
    out,
    fields,
    tiles,
    turned,
    tables,
    stage,
    field_same,
    field_other,
    modes,
    closing,
    part,
    far_part,
    part_in,
    far_in,
    window,
    spread,
    near,
    near_stage,
    near_same,
    near_other,
    back,
    returned,
    back_far,
    returned_far,
    send_sem,
    recv_sem,
    load_sem,
):
    az = lax.axis_index("az")
    curve = lax.axis_index("curve")
    blocks = lax.axis_size("curve")
    half = az // GROUPS
    me = az % GROUPS
    base = half * GROUPS
    far = (1 - half) * GROUPS
    last = blocks - 1
    at_end = jnp.logical_or(curve == 0, curve == last)
    up = (az, (curve + 1) % blocks)
    down = (az, (curve + last) % blocks)
    beyond = jnp.where(curve == 0, last, 0)
    beyond_place = jnp.where(curve == 0, 2, 0)
    beyond_row = jnp.where(curve == 0, HALO_DOWN, HALO_UP)

    def peer(step):
        return (me + step) % GROUPS

    barrier = pltpu.get_barrier_semaphore()

    def greet(device):
        pl.semaphore_signal(barrier, inc=1, device_id=device, device_id_type=MESH)

    for step in range(GROUPS):
        greet((far + peer(step), curve))

    @pl.when(at_end)
    def _():
        for step in range(GROUPS):
            greet((far + peer(step), beyond))

    @pl.when(curve != last)
    def _():
        greet(up)

    @pl.when(curve != 0)
    def _():
        greet(down)

    for step in range(1, GROUPS):
        greet((base + peer(step), curve))

    def field_load(chunk):
        rows = pl.ds(chunk * GROUPS, GROUPS)
        return pltpu.make_async_copy(fields_hbm.at[:, rows], fields.at[chunk], load_sem.at[5 + chunk])

    for chunk in range(CHUNKS):
        field_load(chunk).start()
    table_load = pltpu.make_async_copy(tables_hbm, tables, load_sem.at[1])
    table_load.start()
    tile_load = pltpu.make_async_copy(tiles_hbm, tiles, load_sem.at[2])
    tile_load.start()

    def remote(source, target, row, chunk, device):
        pltpu.make_async_remote_copy(
            src_ref=source,
            dst_ref=target,
            send_sem=send_sem.at[row, chunk],
            recv_sem=recv_sem.at[row, chunk],
            device_id=device,
            device_id_type=MESH,
        ).start()

    def take(ref, row, chunk):
        pltpu.make_async_copy(ref, ref, recv_sem.at[row, chunk]).wait()

    def drain(ref, row, chunk):
        pltpu.make_async_copy(ref, ref, send_sem.at[row, chunk]).wait()

    def send_same(source, same, row, chunk):
        for step in range(1, GROUPS):
            group = peer(step)
            remote(source.at[chunk, group], same.at[chunk, :, me], row, chunk, (base + group, curve))
        same[chunk, 0, me] = source[chunk, me, 0]
        same[chunk, 1, me] = source[chunk, me, 1]

    def send_other(source, other, row, chunk):
        for step in range(GROUPS):
            group = peer(step)
            remote(source.at[chunk, group, 0], other.at[me], row, chunk, (far + group, curve))

    def rows_of(value):
        return value.reshape(GROUPS * 2 * LOCAL, value.shape[-1])

    width = GROUPS * 2 * LOCAL

    def transform_same(same, chunk, side, first):
        columns = pl.ds(first * width, width)
        high = rows_of(same[chunk, 0])
        low = rows_of(same[chunk, 1])
        return (
            dot(tables[side, 0, :, columns], high)
            + dot(tables[side, 0, :, columns], low)
            + dot(tables[side, 1, :, columns], high)
        )

    def transform_other(other, side, first):
        columns = pl.ds(first * width, width)
        high = rows_of(other[...])
        return dot(tables[side, 0, :, columns], high) + dot(tables[side, 1, :, columns], high)

    def fill(chunk):
        field_load(chunk).wait()
        for group in range(GROUPS):
            high, low = split(fields[chunk, :, group, :])
            stage[chunk, group, 0] = high
            stage[chunk, group, 1] = low

    fill(0)
    fill(1)
    pl.semaphore_wait(barrier, jnp.where(at_end, 3 * GROUPS, 2 * GROUPS + 1))
    send_other(stage, field_other.at[0], FIELD_OTHER, 0)
    send_same(stage, field_same, FIELD, 1)

    @pl.when(at_end)
    def _():
        send_other(stage, field_other.at[1], FIELD_OTHER, 1)

    send_same(stage, field_same, FIELD, 0)
    table_load.wait()

    scale = 1.0 / (2 * GROUPS * LOCAL)

    def settled(total):
        return (total * scale).astype(BF16)

    def forward_first(chunk):
        take(field_same.at[chunk, :, pl.ds(0, GROUPS - 1)], FIELD, chunk)
        total = transform_same(field_same, chunk, half, 0)
        take(field_other.at[chunk], FIELD_OTHER, chunk)
        total = total + transform_other(field_other.at[chunk], half, 1)
        modes[...] = settled(total).reshape(modes.shape)
        for step in range(1, GROUPS):
            group = peer(step)
            remote(modes.at[group], window.at[chunk, 1, me], MODE_OWN, chunk, (base + group, curve))
        window[chunk, 1, me] = modes[me]

    def forward_last(chunk):
        take(field_same.at[chunk, :, pl.ds(0, GROUPS - 1)], FIELD, chunk)
        theirs = transform_same(field_same, chunk, 1 - half, 1)
        far_part[...] = theirs.astype(BF16).reshape(far_part.shape)
        for step in range(GROUPS):
            group = peer(step)
            remote(far_part.at[group], far_in.at[me], FAR_PART, chunk, (far + group, curve))
        ours = transform_same(field_same, chunk, half, 0)
        part[...] = ours.reshape(part.shape)
        for step in range(1, GROUPS):
            group = peer(step)
            remote(part.at[group], part_in.at[me], PART, chunk, (base + group, curve))
        part_in[me] = part[me]

    def close(chunk):
        @pl.when(at_end)
        def _():
            if chunk == 1:
                take(field_other.at[chunk], FIELD_OTHER, chunk)
            total = transform_same(field_same, chunk, 1 - half, 1)
            total = total + transform_other(field_other.at[chunk], 1 - half, 0)
            closing[chunk] = settled(total).reshape(closing.shape[1:])
            for step in range(GROUPS):
                group = peer(step)
                target = window.at[chunk, beyond_place, me]
                remote(closing.at[chunk, group], target, beyond_row, chunk, (far + group, beyond))

    def halo(chunk):
        if chunk == 0:
            take(window.at[chunk, 1, pl.ds(0, GROUPS - 1)], MODE_OWN, chunk)
        else:
            take(part_in.at[pl.ds(0, GROUPS - 1)], PART, chunk)
            take(far_in, FAR_PART, chunk)
            window[chunk, 1] = settled(part_in[...] + far_in[...].astype(F32))

        @pl.when(curve != last)
        def _():
            remote(window.at[chunk, 1], window.at[chunk, 0], HALO_UP, chunk, up)

        @pl.when(curve != 0)
        def _():
            remote(window.at[chunk, 1], window.at[chunk, 2], HALO_DOWN, chunk, down)

    def slot_of(mode, place):
        block = (curve + place + last) % blocks
        slot = jnp.where(cols_ref[0, 0, mode] == block, 0, jnp.where(cols_ref[1, 0, mode] == block, 1, 2))
        return slot, jnp.where(slot < count_ref[mode], 1.0, 0.0).astype(F32)

    def prepare():
        def body(mode, carry):
            for index, place in enumerate((1, 0, 2)):
                slot, weight = slot_of(mode, place)
                for kind in range(2):
                    tile = tiles[mode, slot, kind].astype(F32) * weight
                    turned[mode, index, kind] = jnp.transpose(tile).astype(BF16)
            return carry

        lax.fori_loop(0, LOCAL, body, 0)

    def spectrum_rows(mode, place):
        real = spread[place, pl.ds(mode, GROUPS, stride=2 * LOCAL), :]
        minus_imag = -spread[place, pl.ds(mode + LOCAL, GROUPS, stride=2 * LOCAL), :]
        left = jnp.concatenate([real, minus_imag], axis=0)
        right = jnp.concatenate([minus_imag, -real], axis=0)
        return [left.astype(BF16), right.astype(BF16)]

    def product(mode, places, first):
        left = jnp.concatenate([part for place in places for part in spectrum_rows(mode, place)], axis=1)
        right = turned[mode, pl.ds(first, len(places))]
        return dot(left, right.reshape(left.shape[1], right.shape[-1]))

    unroll = 4

    def near_own(chunk):
        spread[1] = rows_of(window[chunk, 1]).astype(F32)

        def body(index, carry):
            for inner in range(unroll):
                mode = index * unroll + inner
                total = product(mode, (1,), 0)
                near[chunk, pl.ds(mode, GROUPS, stride=2 * LOCAL), :] = total[:GROUPS]
                near[chunk, pl.ds(mode + LOCAL, GROUPS, stride=2 * LOCAL), :] = total[GROUPS:]
            return carry

        lax.fori_loop(0, LOCAL // unroll, body, 0)

    def near_rest(chunk):
        take(window.at[chunk, 0], HALO_UP, chunk)
        take(window.at[chunk, 2], HALO_DOWN, chunk)
        spread[0] = rows_of(window[chunk, 0]).astype(F32)
        spread[2] = rows_of(window[chunk, 2]).astype(F32)

        def body(index, carry):
            for inner in range(unroll):
                mode = index * unroll + inner
                total = product(mode, (0, 2), 1)
                real = pl.ds(mode, GROUPS, stride=2 * LOCAL)
                imag = pl.ds(mode + LOCAL, GROUPS, stride=2 * LOCAL)
                near[chunk, real, :] = near[chunk, real, :] + total[:GROUPS]
                near[chunk, imag, :] = near[chunk, imag, :] + total[GROUPS:]
            return carry

        lax.fori_loop(0, LOCAL // unroll, body, 0)
        high, low = split(near[chunk])
        near_stage[chunk, :, 0] = high.reshape(GROUPS, 2 * LOCAL, high.shape[-1])
        near_stage[chunk, :, 1] = low.reshape(GROUPS, 2 * LOCAL, low.shape[-1])
        if chunk == 0:
            send_other(near_stage, near_other, NEAR_OTHER, chunk)
            send_same(near_stage, near_same, NEAR_SAME, chunk)
        else:
            send_same(near_stage, near_same, NEAR_SAME, chunk)

    mine = pl.ds(pl.multiple_of(me * 2 * LOCAL, 2 * LOCAL), 2 * LOCAL)

    def send_back(total, chunk):
        back[chunk] = total.reshape(back.shape[1:])
        for step in range(1, GROUPS):
            group = peer(step)
            remote(back.at[chunk, group], returned.at[chunk, mine], BACK, chunk, (base + group, curve))
        returned[chunk, mine] = back[chunk, me]

    def inverse_first(chunk):
        take(near_same.at[chunk, :, pl.ds(0, GROUPS - 1)], NEAR_SAME, chunk)
        total = transform_same(near_same, chunk, half, 0)
        take(near_other, NEAR_OTHER, chunk)
        send_back(total + transform_other(near_other, half, 1), chunk)

    def inverse_last(chunk):
        take(near_same.at[chunk, :, pl.ds(0, GROUPS - 1)], NEAR_SAME, chunk)
        theirs = transform_same(near_same, chunk, 1 - half, 1)
        back_far[...] = theirs.astype(BF16).reshape(back_far.shape)
        for step in range(GROUPS):
            group = peer(step)
            remote(back_far.at[group], returned_far.at[me], BACK_FAR, chunk, (far + group, curve))
        send_back(transform_same(near_same, chunk, half, 0), chunk)

    def combine(chunk):
        take(returned.at[chunk, pl.ds(0, (GROUPS - 1) * 2 * LOCAL)], BACK, chunk)
        if chunk > 0:
            take(returned_far, BACK_FAR, chunk)
            returned[chunk] = returned[chunk] + rows_of(returned_far[...]).astype(F32)
        for point in range(LOCAL):
            real = returned[chunk, pl.ds(point, GROUPS, stride=2 * LOCAL), :]
            minus_imag = returned[chunk, pl.ds(point + LOCAL, GROUPS, stride=2 * LOCAL), :]
            imped_real = imped_ref[pl.ds(point, 1), :]
            imped_imag = imped_ref[pl.ds(point + LOCAL, 1), :]
            rows = pl.ds(chunk * GROUPS, GROUPS)
            out[point, rows, :] = imped_real * real + imped_imag * minus_imag
            out[point + LOCAL, rows, :] = imped_imag * real - imped_real * minus_imag

    forward_last(1)
    tile_load.wait()
    prepare()
    forward_first(0)
    close(0)
    halo(0)
    close(1)
    halo(1)
    near_own(0)
    near_own(1)
    near_rest(0)
    near_rest(1)
    inverse_last(1)
    inverse_first(0)
    combine(0)
    combine(1)

    drain(field_other.at[0], FIELD_OTHER, 0)
    drain(window.at[0, 1, pl.ds(0, GROUPS - 1)], MODE_OWN, 0)
    drain(far_in, FAR_PART, 1)
    drain(part_in.at[pl.ds(0, GROUPS - 1)], PART, 1)

    @pl.when(at_end)
    def _():
        drain(field_other.at[1], FIELD_OTHER, 1)

    for chunk in range(CHUNKS):
        drain(field_same.at[chunk, :, pl.ds(0, GROUPS - 1)], FIELD, chunk)
        drain(window.at[chunk, 0], HALO_UP, chunk)
        drain(window.at[chunk, 2], HALO_DOWN, chunk)
        drain(near_same.at[chunk, :, pl.ds(0, GROUPS - 1)], NEAR_SAME, chunk)
        if chunk == 0:
            drain(near_other, NEAR_OTHER, chunk)
        else:
            drain(returned_far, BACK_FAR, chunk)
        drain(returned.at[chunk, pl.ds(0, (GROUPS - 1) * 2 * LOCAL)], BACK, chunk)


def on_device(tables, fields, impedance, tile_data, tile_cols, tile_count):
    points, rhs, nodes = fields.shape[1:]
    block = tile_data.shape[-1]
    modes, _, slots = tile_data.shape[:3]
    pair = 2 * LOCAL
    whole = GROUPS * pair
    vmem = pl.BlockSpec(memory_space=pltpu.VMEM)
    smem = pl.BlockSpec(memory_space=pltpu.SMEM)
    hbm = pl.BlockSpec(memory_space=pl.ANY)
    out = pl.pallas_call(
        kernel,
        out_shape=pltpu.VMEM((2 * points, rhs, nodes), F32),
        in_specs=[hbm, vmem, smem, smem, hbm, hbm],
        out_specs=vmem,
        scratch_shapes=[
            pltpu.VMEM((CHUNKS, 2 * points, GROUPS, nodes), F32),
            pltpu.VMEM((modes, slots, 2, block, block), BF16),
            pltpu.VMEM((modes, slots, 2, block, block), BF16),
            pltpu.VMEM(tables.shape, BF16),
            pltpu.VMEM((CHUNKS, GROUPS, 2, pair, nodes), BF16),
            pltpu.VMEM((CHUNKS, 2, GROUPS, pair, nodes), BF16),
            pltpu.VMEM((CHUNKS, GROUPS, pair, nodes), BF16),
            pltpu.VMEM((GROUPS, pair, nodes), BF16),
            pltpu.VMEM((CHUNKS, GROUPS, pair, nodes), BF16),
            pltpu.VMEM((GROUPS, pair, nodes), F32),
            pltpu.VMEM((GROUPS, pair, nodes), BF16),
            pltpu.VMEM((GROUPS, pair, nodes), F32),
            pltpu.VMEM((GROUPS, pair, nodes), BF16),
            pltpu.VMEM((CHUNKS, 3, GROUPS, pair, nodes), BF16),
            pltpu.VMEM((3, whole, nodes), F32),
            pltpu.VMEM((CHUNKS, whole, nodes), F32),
            pltpu.VMEM((CHUNKS, GROUPS, 2, pair, nodes), BF16),
            pltpu.VMEM((CHUNKS, 2, GROUPS, pair, nodes), BF16),
            pltpu.VMEM((GROUPS, pair, nodes), BF16),
            pltpu.VMEM((CHUNKS, GROUPS, pair, nodes), F32),
            pltpu.VMEM((CHUNKS, whole, nodes), F32),
            pltpu.VMEM((GROUPS, pair, nodes), BF16),
            pltpu.VMEM((GROUPS, pair, nodes), BF16),
            pltpu.SemaphoreType.DMA((11, CHUNKS)),
            pltpu.SemaphoreType.DMA((11, CHUNKS)),
            pltpu.SemaphoreType.DMA((3 + 2 * CHUNKS,)),
        ],
        compiler_params=pltpu.CompilerParams(collective_id=0, has_side_effects=True),
    )(
        fields.reshape(2 * points, rhs, nodes),
        impedance.reshape(2 * points, nodes),
        jnp.transpose(tile_cols, (2, 1, 0)),
        tile_count.reshape(modes),
        tile_data.reshape(modes, slots, 2, block, block),
        tables,
    )
    return fields + out.reshape(fields.shape)


def solution(mesh):
    placed = (
        P(None, "az", None, "curve"),
        P(None, "az", "curve"),
        P("az", "curve", None, None, None, None),
        P("az", "curve", None),
        P("az", "curve"),
    )

    def apply(*arrays):
        tables = jnp.asarray(transform_tables())
        return jax.shard_map(
            on_device,
            mesh=mesh,
            in_specs=(P(),) + placed,
            out_specs=P(None, "az", None, "curve"),
            check_vma=False,
        )(tables, *arrays)

    return apply
```

```python
import functools
import math

import jax
import jax.numpy as jnp
import numpy as np
from jax import lax
from jax.experimental import pallas as pl
from jax.experimental.pallas import tpu as pltpu
from jax.sharding import PartitionSpec as P

MESH = pl.DeviceIdType.MESH
F32 = jnp.float32
BF16 = jnp.bfloat16
FIELD, FIELD_OTHER, MODE_OWN, PART, FAR_PART = range(5)
HALO_UP, HALO_DOWN, NEAR_SAME, NEAR_OTHER, BACK, BACK_FAR = range(5, 11)
CHUNKS = 2
GROUPS = 8
LOCAL = 16


def transform_tables():
    period = 2 * GROUPS * LOCAL
    half_size = GROUPS * LOCAL
    tables = []
    for half in range(2):
        k = half * half_size + np.arange(half_size).reshape(GROUPS, 1, LOCAL)
        p = np.stack([side * half_size + np.arange(half_size) for side in (half, 1 - half)])
        p = p.reshape(2, GROUPS, 1, LOCAL)
        product = (k.reshape(-1, 1) * p.reshape(1, -1)) % period
        angle = 2.0 * math.pi / period * product
        cosine = np.cos(angle).reshape(GROUPS, LOCAL, 2, GROUPS, LOCAL)
        sine = np.sin(angle).reshape(GROUPS, LOCAL, 2, GROUPS, LOCAL)
        full = np.zeros((GROUPS, 2, LOCAL, 2, GROUPS, 2, LOCAL))
        full[:, 0, :, :, :, 0, :] = cosine
        full[:, 0, :, :, :, 1, :] = sine
        full[:, 1, :, :, :, 0, :] = -sine
        full[:, 1, :, :, :, 1, :] = cosine
        full = full.reshape(2 * half_size, 4 * half_size)
        high = full.astype(np.float32).astype(jnp.bfloat16)
        low = (full - high.astype(np.float64)).astype(np.float32).astype(jnp.bfloat16)
        tables.append(np.stack([high, low]))
    return np.stack(tables)


def dot(left, right):
    return jnp.dot(left, right, preferred_element_type=F32)


def split(value):
    high = value.astype(BF16)
    low = (value - high.astype(F32)).astype(BF16)
    return high, low


def kernel(
    fields_hbm,
    imped_ref,
    cols_ref,
    count_ref,
    tiles_hbm,
    tables_hbm,
    out,
    fields,
    tiles,
    turned,
    tables,
    stage,
    field_same,
    field_other,
    modes,
    closing,
    part,
    far_part,
    part_in,
    far_in,
    window,
    spread,
    near,
    near_stage,
    near_same,
    near_other,
    back,
    returned,
    back_far,
    returned_far,
    send_sem,
    recv_sem,
    load_sem,
):
    az = lax.axis_index("az")
    curve = lax.axis_index("curve")
    blocks = lax.axis_size("curve")
    half = az // GROUPS
    me = az % GROUPS
    base = half * GROUPS
    far = (1 - half) * GROUPS
    last = blocks - 1
    at_end = jnp.logical_or(curve == 0, curve == last)
    up = (az, (curve + 1) % blocks)
    down = (az, (curve + last) % blocks)
    beyond = jnp.where(curve == 0, last, 0)
    beyond_place = jnp.where(curve == 0, 2, 0)
    beyond_row = jnp.where(curve == 0, HALO_DOWN, HALO_UP)

    def peer(step):
        return (me + step) % GROUPS

    barrier = pltpu.get_barrier_semaphore()

    def greet(device):
        pl.semaphore_signal(barrier, inc=1, device_id=device, device_id_type=MESH)

    for step in range(GROUPS):
        greet((far + peer(step), curve))

    @pl.when(at_end)
    def _():
        for step in range(GROUPS):
            greet((far + peer(step), beyond))

    @pl.when(curve != last)
    def _():
        greet(up)

    @pl.when(curve != 0)
    def _():
        greet(down)

    for step in range(1, GROUPS):
        greet((base + peer(step), curve))

    def field_load(chunk):
        rows = pl.ds(chunk * GROUPS, GROUPS)
        return pltpu.make_async_copy(fields_hbm.at[:, rows], fields.at[chunk], load_sem.at[5 + chunk])

    for chunk in range(CHUNKS):
        field_load(chunk).start()
    table_load = pltpu.make_async_copy(tables_hbm, tables, load_sem.at[1])
    table_load.start()
    tile_load = pltpu.make_async_copy(tiles_hbm, tiles, load_sem.at[2])
    tile_load.start()

    def remote(source, target, row, chunk, device):
        pltpu.make_async_remote_copy(
            src_ref=source,
            dst_ref=target,
            send_sem=send_sem.at[row, chunk],
            recv_sem=recv_sem.at[row, chunk],
            device_id=device,
            device_id_type=MESH,
        ).start()

    def take(ref, row, chunk):
        pltpu.make_async_copy(ref, ref, recv_sem.at[row, chunk]).wait()

    def drain(ref, row, chunk):
        pltpu.make_async_copy(ref, ref, send_sem.at[row, chunk]).wait()

    def send_same(source, same, row, chunk):
        for step in range(1, GROUPS):
            group = peer(step)
            remote(source.at[chunk, group], same.at[chunk, :, me], row, chunk, (base + group, curve))
        same[chunk, 0, me] = source[chunk, me, 0]
        same[chunk, 1, me] = source[chunk, me, 1]

    def send_other(source, other, row, chunk):
        for step in range(GROUPS):
            group = peer(step)
            remote(source.at[chunk, group, 0], other.at[me], row, chunk, (far + group, curve))

    def rows_of(value):
        return value.reshape(GROUPS * 2 * LOCAL, value.shape[-1])

    width = GROUPS * 2 * LOCAL

    def transform_same(same, chunk, side, first):
        columns = pl.ds(first * width, width)
        high = rows_of(same[chunk, 0])
        low = rows_of(same[chunk, 1])
        return (
            dot(tables[side, 0, :, columns], high)
            + dot(tables[side, 0, :, columns], low)
            + dot(tables[side, 1, :, columns], high)
        )

    def transform_other(other, side, first):
        columns = pl.ds(first * width, width)
        high = rows_of(other[...])
        return dot(tables[side, 0, :, columns], high) + dot(tables[side, 1, :, columns], high)

    def fill(chunk):
        field_load(chunk).wait()
        for group in range(GROUPS):
            high, low = split(fields[chunk, :, group, :])
            stage[chunk, group, 0] = high
            stage[chunk, group, 1] = low

    fill(0)
    fill(1)
    pl.semaphore_wait(barrier, jnp.where(at_end, 3 * GROUPS, 2 * GROUPS + 1))
    send_other(stage, field_other.at[0], FIELD_OTHER, 0)
    send_same(stage, field_same, FIELD, 1)

    @pl.when(at_end)
    def _():
        send_other(stage, field_other.at[1], FIELD_OTHER, 1)

    send_same(stage, field_same, FIELD, 0)
    table_load.wait()

    scale = 1.0 / (2 * GROUPS * LOCAL)

    def settled(total):
        return (total * scale).astype(BF16)

    def forward_first(chunk):
        take(field_same.at[chunk, :, pl.ds(0, GROUPS - 1)], FIELD, chunk)
        total = transform_same(field_same, chunk, half, 0)
        take(field_other.at[chunk], FIELD_OTHER, chunk)
        total = total + transform_other(field_other.at[chunk], half, 1)
        modes[...] = settled(total).reshape(modes.shape)
        for step in range(1, GROUPS):
            group = peer(step)
            remote(modes.at[group], window.at[chunk, 1, me], MODE_OWN, chunk, (base + group, curve))
        window[chunk, 1, me] = modes[me]

    def forward_last(chunk):
        take(field_same.at[chunk, :, pl.ds(0, GROUPS - 1)], FIELD, chunk)
        theirs = transform_same(field_same, chunk, 1 - half, 1)
        far_part[...] = theirs.astype(BF16).reshape(far_part.shape)
        for step in range(GROUPS):
            group = peer(step)
            remote(far_part.at[group], far_in.at[me], FAR_PART, chunk, (far + group, curve))
        ours = transform_same(field_same, chunk, half, 0)
        part[...] = ours.reshape(part.shape)
        for step in range(1, GROUPS):
            group = peer(step)
            remote(part.at[group], part_in.at[me], PART, chunk, (base + group, curve))
        part_in[me] = part[me]

    def close(chunk):
        @pl.when(at_end)
        def _():
            if chunk == 1:
                take(field_other.at[chunk], FIELD_OTHER, chunk)
            total = transform_same(field_same, chunk, 1 - half, 1)
            total = total + transform_other(field_other.at[chunk], 1 - half, 0)
            closing[chunk] = settled(total).reshape(closing.shape[1:])
            for step in range(GROUPS):
                group = peer(step)
                target = window.at[chunk, beyond_place, me]
                remote(closing.at[chunk, group], target, beyond_row, chunk, (far + group, beyond))

    def halo(chunk):
        if chunk == 0:
            take(window.at[chunk, 1, pl.ds(0, GROUPS - 1)], MODE_OWN, chunk)
        else:
            take(part_in.at[pl.ds(0, GROUPS - 1)], PART, chunk)
            take(far_in, FAR_PART, chunk)
            window[chunk, 1] = settled(part_in[...] + far_in[...].astype(F32))

        @pl.when(curve != last)
        def _():
            remote(window.at[chunk, 1], window.at[chunk, 0], HALO_UP, chunk, up)

        @pl.when(curve != 0)
        def _():
            remote(window.at[chunk, 1], window.at[chunk, 2], HALO_DOWN, chunk, down)

    def slot_of(mode, place):
        block = (curve + place + last) % blocks
        slot = jnp.where(cols_ref[0, 0, mode] == block, 0, jnp.where(cols_ref[1, 0, mode] == block, 1, 2))
        return slot, jnp.where(slot < count_ref[mode], 1.0, 0.0).astype(F32)

    def prepare():
        def body(mode, carry):
            for index, place in enumerate((1, 0, 2)):
                slot, weight = slot_of(mode, place)
                for kind in range(2):
                    tile = tiles[mode, slot, kind].astype(F32) * weight
                    turned[mode, index, kind] = jnp.transpose(tile).astype(BF16)
            return carry

        lax.fori_loop(0, LOCAL, body, 0)

    def spectrum_rows(mode, place):
        real = spread[place, pl.ds(mode, GROUPS, stride=2 * LOCAL), :]
        minus_imag = -spread[place, pl.ds(mode + LOCAL, GROUPS, stride=2 * LOCAL), :]
        left = jnp.concatenate([real, minus_imag], axis=0)
        right = jnp.concatenate([minus_imag, -real], axis=0)
        return [left.astype(BF16), right.astype(BF16)]

    def product(mode, places, first):
        left = jnp.concatenate([part for place in places for part in spectrum_rows(mode, place)], axis=1)
        right = turned[mode, pl.ds(first, len(places))]
        return dot(left, right.reshape(left.shape[1], right.shape[-1]))

    unroll = 4

    def near_own(chunk):
        spread[1] = rows_of(window[chunk, 1]).astype(F32)

        def body(index, carry):
            for inner in range(unroll):
                mode = index * unroll + inner
                total = product(mode, (1,), 0)
                near[chunk, pl.ds(mode, GROUPS, stride=2 * LOCAL), :] = total[:GROUPS]
                near[chunk, pl.ds(mode + LOCAL, GROUPS, stride=2 * LOCAL), :] = total[GROUPS:]
            return carry

        lax.fori_loop(0, LOCAL // unroll, body, 0)

    def near_rest(chunk):
        take(window.at[chunk, 0], HALO_UP, chunk)
        take(window.at[chunk, 2], HALO_DOWN, chunk)
        spread[0] = rows_of(window[chunk, 0]).astype(F32)
        spread[2] = rows_of(window[chunk, 2]).astype(F32)

        def body(index, carry):
            for inner in range(unroll):
                mode = index * unroll + inner
                total = product(mode, (0, 2), 1)
                real = pl.ds(mode, GROUPS, stride=2 * LOCAL)
                imag = pl.ds(mode + LOCAL, GROUPS, stride=2 * LOCAL)
                near[chunk, real, :] = near[chunk, real, :] + total[:GROUPS]
                near[chunk, imag, :] = near[chunk, imag, :] + total[GROUPS:]
            return carry

        lax.fori_loop(0, LOCAL // unroll, body, 0)
        high, low = split(near[chunk])
        near_stage[chunk, :, 0] = high.reshape(GROUPS, 2 * LOCAL, high.shape[-1])
        near_stage[chunk, :, 1] = low.reshape(GROUPS, 2 * LOCAL, low.shape[-1])
        if chunk == 0:
            send_other(near_stage, near_other, NEAR_OTHER, chunk)
            send_same(near_stage, near_same, NEAR_SAME, chunk)
        else:
            send_same(near_stage, near_same, NEAR_SAME, chunk)

    mine = pl.ds(pl.multiple_of(me * 2 * LOCAL, 2 * LOCAL), 2 * LOCAL)

    def send_back(total, chunk):
        back[chunk] = total.reshape(back.shape[1:])
        for step in range(1, GROUPS):
            group = peer(step)
            remote(back.at[chunk, group], returned.at[chunk, mine], BACK, chunk, (base + group, curve))
        returned[chunk, mine] = back[chunk, me]

    def inverse_first(chunk):
        take(near_same.at[chunk, :, pl.ds(0, GROUPS - 1)], NEAR_SAME, chunk)
        total = transform_same(near_same, chunk, half, 0)
        take(near_other, NEAR_OTHER, chunk)
        send_back(total + transform_other(near_other, half, 1), chunk)

    def inverse_last(chunk):
        take(near_same.at[chunk, :, pl.ds(0, GROUPS - 1)], NEAR_SAME, chunk)
        theirs = transform_same(near_same, chunk, 1 - half, 1)
        back_far[...] = theirs.astype(BF16).reshape(back_far.shape)
        for step in range(GROUPS):
            group = peer(step)
            remote(back_far.at[group], returned_far.at[me], BACK_FAR, chunk, (far + group, curve))
        send_back(transform_same(near_same, chunk, half, 0), chunk)

    def combine(chunk):
        take(returned.at[chunk, pl.ds(0, (GROUPS - 1) * 2 * LOCAL)], BACK, chunk)
        if chunk > 0:
            take(returned_far, BACK_FAR, chunk)
            returned[chunk] = returned[chunk] + rows_of(returned_far[...]).astype(F32)
        for point in range(LOCAL):
            real = returned[chunk, pl.ds(point, GROUPS, stride=2 * LOCAL), :]
            minus_imag = returned[chunk, pl.ds(point + LOCAL, GROUPS, stride=2 * LOCAL), :]
            imped_real = imped_ref[pl.ds(point, 1), :]
            imped_imag = imped_ref[pl.ds(point + LOCAL, 1), :]
            rows = pl.ds(chunk * GROUPS, GROUPS)
            out[point, rows, :] = fields[chunk, point] + imped_real * real + imped_imag * minus_imag
            out[point + LOCAL, rows, :] = fields[chunk, point + LOCAL] + imped_imag * real - imped_real * minus_imag

    forward_last(1)
    tile_load.wait()
    prepare()
    forward_first(0)
    close(0)
    halo(0)
    close(1)
    halo(1)
    near_own(0)
    near_own(1)
    near_rest(0)
    near_rest(1)
    inverse_last(1)
    inverse_first(0)
    combine(0)
    combine(1)

    drain(field_other.at[0], FIELD_OTHER, 0)
    drain(window.at[0, 1, pl.ds(0, GROUPS - 1)], MODE_OWN, 0)
    drain(far_in, FAR_PART, 1)
    drain(part_in.at[pl.ds(0, GROUPS - 1)], PART, 1)

    @pl.when(at_end)
    def _():
        drain(field_other.at[1], FIELD_OTHER, 1)

    for chunk in range(CHUNKS):
        drain(field_same.at[chunk, :, pl.ds(0, GROUPS - 1)], FIELD, chunk)
        drain(window.at[chunk, 0], HALO_UP, chunk)
        drain(window.at[chunk, 2], HALO_DOWN, chunk)
        drain(near_same.at[chunk, :, pl.ds(0, GROUPS - 1)], NEAR_SAME, chunk)
        if chunk == 0:
            drain(near_other, NEAR_OTHER, chunk)
        else:
            drain(returned_far, BACK_FAR, chunk)
        drain(returned.at[chunk, pl.ds(0, (GROUPS - 1) * 2 * LOCAL)], BACK, chunk)


def on_device(tables, fields, impedance, tile_data, tile_cols, tile_count):
    points, rhs, nodes = fields.shape[1:]
    block = tile_data.shape[-1]
    modes, _, slots = tile_data.shape[:3]
    pair = 2 * LOCAL
    whole = GROUPS * pair
    vmem = pl.BlockSpec(memory_space=pltpu.VMEM)
    smem = pl.BlockSpec(memory_space=pltpu.SMEM)
    hbm = pl.BlockSpec(memory_space=pl.ANY)
    out = pl.pallas_call(
        kernel,
        out_shape=pltpu.VMEM((2 * points, rhs, nodes), F32),
        in_specs=[hbm, vmem, smem, smem, hbm, hbm],
        out_specs=vmem,
        scratch_shapes=[
            pltpu.VMEM((CHUNKS, 2 * points, GROUPS, nodes), F32),
            pltpu.VMEM((modes, slots, 2, block, block), BF16),
            pltpu.VMEM((modes, slots, 2, block, block), BF16),
            pltpu.VMEM(tables.shape, BF16),
            pltpu.VMEM((CHUNKS, GROUPS, 2, pair, nodes), BF16),
            pltpu.VMEM((CHUNKS, 2, GROUPS, pair, nodes), BF16),
            pltpu.VMEM((CHUNKS, GROUPS, pair, nodes), BF16),
            pltpu.VMEM((GROUPS, pair, nodes), BF16),
            pltpu.VMEM((CHUNKS, GROUPS, pair, nodes), BF16),
            pltpu.VMEM((GROUPS, pair, nodes), F32),
            pltpu.VMEM((GROUPS, pair, nodes), BF16),
            pltpu.VMEM((GROUPS, pair, nodes), F32),
            pltpu.VMEM((GROUPS, pair, nodes), BF16),
            pltpu.VMEM((CHUNKS, 3, GROUPS, pair, nodes), BF16),
            pltpu.VMEM((3, whole, nodes), F32),
            pltpu.VMEM((CHUNKS, whole, nodes), F32),
            pltpu.VMEM((CHUNKS, GROUPS, 2, pair, nodes), BF16),
            pltpu.VMEM((CHUNKS, 2, GROUPS, pair, nodes), BF16),
            pltpu.VMEM((GROUPS, pair, nodes), BF16),
            pltpu.VMEM((CHUNKS, GROUPS, pair, nodes), F32),
            pltpu.VMEM((CHUNKS, whole, nodes), F32),
            pltpu.VMEM((GROUPS, pair, nodes), BF16),
            pltpu.VMEM((GROUPS, pair, nodes), BF16),
            pltpu.SemaphoreType.DMA((11, CHUNKS)),
            pltpu.SemaphoreType.DMA((11, CHUNKS)),
            pltpu.SemaphoreType.DMA((3 + 2 * CHUNKS,)),
        ],
        compiler_params=pltpu.CompilerParams(collective_id=0, has_side_effects=True),
    )(
        fields.reshape(2 * points, rhs, nodes),
        impedance.reshape(2 * points, nodes),
        jnp.transpose(tile_cols, (2, 1, 0)),
        tile_count.reshape(modes),
        tile_data.reshape(modes, slots, 2, block, block),
        tables,
    )
    return out.reshape(fields.shape)


def solution(mesh):
    placed = (
        P(None, "az", None, "curve"),
        P(None, "az", "curve"),
        P("az", "curve", None, None, None, None),
        P("az", "curve", None),
        P("az", "curve"),
    )

    def apply(*arrays):
        tables = jnp.asarray(transform_tables())
        return jax.shard_map(
            on_device,
            mesh=mesh,
            in_specs=(P(),) + placed,
            out_specs=P(None, "az", None, "curve"),
            check_vma=False,
        )(tables, *arrays)

    return apply
```
